32 devices in a mesh: smp: 8 (over z, y), par: 4 (over x, core).
Axes of the slice: x: 2, y: 2, z: 4, core: 2. Of those that a mesh axis runs over, the one named last changes fastest.
Arguments:
- derivatives: bfloat16 [640, 2048], P('smp', 'par'), may hold values from -40 to 40
- epsilon: float32 [640], P('smp'), may hold values from -6 to 6
Outputs:
- gram_tile: float32 [640, 640], P('smp', 'par')
- update: float32 [2048], P('par')
The draws below stay inside these ranges and needn't reach their ends.
All inputs are finite; a program needn't handle non-finite values.
Results may differ from the reference program's by a relative error of at most 0.003.
Values may be sent and summed in bfloat16 or wider, within the bound.
No kernel may reach another device: no remote copies, remote signals or barrier semaphores. Data moves between devices by JAX's collectives and lax.ppermute only.
A program may use at most 64 MiB of HBM per device.

```python
import math
import jax
import jax.numpy as jnp
from jax import lax

P_SIZE = 2048
SAMPLES = 640


def draw_derivatives(key, part):
    keys = jax.random.split(key, 3)
    noise = jnp.clip(jax.random.normal(keys[0], (SAMPLES, P_SIZE), jnp.float32), -6.0, 6.0)
    row_scale = jnp.exp(jax.random.uniform(keys[1], (SAMPLES, 1), jnp.float32, math.log(0.5), math.log(5.0)))
    column_base = jax.random.uniform(keys[2], (1, P_SIZE), jnp.float32, -1.5, 1.5)
    ramp = 1.0 + 2.0 * jnp.arange(SAMPLES, dtype=jnp.float32)[:, None] / SAMPLES
    values = noise * row_scale + column_base * ramp
    return values.astype(jnp.bfloat16)


def levels(own_key, dims, pieces, least, largest):
    level, own = 1.0, jax.random.fold_in(own_key, 6)
    for axis_at, shards_of in pieces:
        steps = jnp.exp(jax.random.uniform(jax.random.fold_in(own, axis_at), (shards_of,), jnp.float32, least / len(pieces), largest / len(pieces)))
        level = level * jnp.repeat(steps, dims[axis_at] // shards_of).reshape([-1 if axis == axis_at else 1 for axis in range(len(dims))])
    return level


def normal_values(key, shape, scale, most, cuts=(), held_as=jnp.bfloat16):
    values = jax.random.normal(key, shape, jnp.float32) * scale
    if len(cuts) > 0:
        values = levels(key, shape, cuts, -0.22, 0.18) * values
    return jnp.clip(values, min=-most, max=most).astype(held_as)


def setup_inputs(seed: int = 0) -> dict:
    key_of = jax.random.split(jax.random.key(seed), 3)
    derivatives = draw_derivatives(jax.random.fold_in(key_of[2], 71), 0)
    epsilon = normal_values(key_of[1], (SAMPLES,), 1.0, 6.0, ((0, 8),), jnp.float32)
    return {"derivatives": derivatives, "epsilon": epsilon}


def reference(derivatives, epsilon):
    widened = derivatives.astype(jnp.float32)
    column_mean = lax.optimization_barrier(jnp.sum(widened, axis=0)) / SAMPLES
    factor = 1.0 / math.sqrt(SAMPLES)
    centered = ((widened - column_mean) * factor).astype(jnp.bfloat16)
    gram_tile = jnp.dot(centered, centered.T, preferred_element_type=jnp.float32)
    update = jnp.dot(epsilon, centered.astype(jnp.float32), precision=lax.Precision.HIGHEST)
    return (gram_tile, update)
```

```python
import functools
import math

import jax
import jax.numpy as jnp
from jax import lax
from jax.experimental import pallas as pl
from jax.experimental.pallas import tpu as pltpu
from jax.sharding import PartitionSpec as P


EXTRA = 8
GRANT = 8 << 20
DIRECT = 8


def centered(values, mean, factor):
    return ((values.astype(jnp.float32) - mean) * factor).astype(jnp.bfloat16)


def pack_kernel(rows, derivatives_ref, epsilon_ref, packed_ref):
    packed_ref[:rows, :] = derivatives_ref[...]
    left = epsilon_ref[...]
    packed_ref[rows:, :] = jnp.zeros((EXTRA, packed_ref.shape[1]), jnp.bfloat16)
    parts = []
    for _ in range(3):
        part = left.astype(jnp.bfloat16)
        left = left - part.astype(jnp.float32)
        parts.append(part.astype(jnp.float32))
    parts.append(jnp.zeros((EXTRA - 3, rows), jnp.float32))
    packed_ref[rows:, :rows] = jnp.concatenate(parts, axis=0).astype(jnp.bfloat16)


def pack(derivatives, epsilon):
    rows, columns = derivatives.shape
    return pl.pallas_call(
        functools.partial(pack_kernel, rows),
        out_shape=jax.ShapeDtypeStruct((rows + EXTRA, columns), jnp.bfloat16),
        compiler_params=pltpu.CompilerParams(vmem_limit_bytes=GRANT),
        name="pack",
    )(derivatives, epsilon.reshape(1, rows))


def tile_kernel(n, m, rows, total_rows, *refs):
    blocks, (kept_ref, sent_ref, update_ref, held, sums) = refs[:n], refs[n:]
    me = lax.axis_index("smp")
    mine = lax.axis_index("par")
    per = n // m
    factor = 1.0 / math.sqrt(total_rows)
    for step, block in enumerate(blocks):
        source = jnp.bitwise_xor(me, step)
        sums[pl.ds(source, 1), :] = jnp.sum(block[:rows, :].astype(jnp.float32), axis=0, keepdims=True)
    mean = jnp.sum(sums[...], axis=0, keepdims=True) / total_rows
    own = None
    for step, block in enumerate(blocks):
        terms = centered(block[:rows, :], mean, factor)
        own = terms if step == 0 else own
        source = jnp.bitwise_xor(me, step)
        place = jnp.bitwise_xor(source // per, mine) * per + source % per
        held[pl.ds(pl.multiple_of(place * rows, rows), rows), :] = terms
        update = jnp.dot(block[rows:, :rows], terms, preferred_element_type=jnp.float32)
        sums[pl.ds(source, 1), :] = jnp.sum(update, axis=0, keepdims=True)
    update_ref[...] = jnp.sum(sums[...], axis=0, keepdims=True)
    half = (n // 2) * rows
    contract = (((1,), (1,)), ((), ()))
    sent_ref[...] = lax.dot_general(own, held[half:, :], contract, preferred_element_type=jnp.float32).astype(jnp.bfloat16)
    kept_ref[...] = lax.dot_general(own, held[:half, :], contract, preferred_element_type=jnp.float32)


def tiles(blocks, m, rows, total_rows):
    n, columns = len(blocks), blocks[0].shape[1]
    half = (n // 2) * rows
    return pl.pallas_call(
        functools.partial(tile_kernel, n, m, rows, total_rows),
        out_shape=(
            jax.ShapeDtypeStruct((rows, half), jnp.float32),
            jax.ShapeDtypeStruct((rows, half), jnp.bfloat16),
            jax.ShapeDtypeStruct((1, columns), jnp.float32),
        ),
        scratch_shapes=[pltpu.VMEM((n * rows, columns), jnp.bfloat16), pltpu.VMEM((n, columns), jnp.float32)],
        compiler_params=pltpu.CompilerParams(vmem_limit_bytes=GRANT),
        name="tiles",
    )(*blocks)


def swap(value, axis, bit):
    return lax.ppermute(value, axis, [(i, i ^ bit) for i in range(lax.axis_size(axis))])


ORDER = ((0, 4), (0, 2), (0, 1), (4, 2), (2, 1), (4, 1), (6, 1))


def direct(derivatives, epsilon):
    n, m = lax.axis_size("smp"), lax.axis_size("par")
    rows = derivatives.shape[0]
    blocks = {0: pack(derivatives, epsilon)}
    for source, bit in ORDER:
        blocks[source ^ bit] = swap(blocks[source], "smp", bit)
    kept, sent, update = tiles([blocks[step] for step in range(n)], m, rows, rows * n)
    both = kept + swap(sent, "par", 2).astype(jnp.float32)
    width = rows * n // m
    gram_tile = both[:, :width] + swap(both[:, width:], "par", 1)
    return (gram_tile, update.reshape(-1))


def gathered(derivatives, epsilon):
    total_rows = derivatives.shape[0] * lax.axis_size("smp")
    factor = 1.0 / math.sqrt(total_rows)
    everything = lax.all_gather(derivatives, "smp", axis=0, tiled=True)
    mean = jnp.sum(everything.astype(jnp.float32), axis=0) / total_rows
    own = centered(derivatives, mean, factor)
    partial_terms = jnp.dot(own, centered(everything, mean, factor).T, preferred_element_type=jnp.float32)
    gram_tile = lax.psum_scatter(partial_terms, "par", scatter_dimension=1, tiled=True)
    local_sum = jnp.dot(epsilon, own.astype(jnp.float32), precision=lax.Precision.HIGHEST)
    return (gram_tile, lax.psum(local_sum, "smp"))


def shards(derivatives, epsilon):
    n, m = lax.axis_size("smp"), lax.axis_size("par")
    if n == DIRECT and m == 4:
        return direct(derivatives, epsilon)
    return gathered(derivatives, epsilon)


def solution(mesh):
    in_specs = (P("smp", "par"), P("smp"))
    out_specs = (P("smp", "par"), P("par"))
    return jax.shard_map(shards, mesh=mesh, in_specs=in_specs, out_specs=out_specs, check_vma=False)
```

```python
import functools
import math

import jax
import jax.numpy as jnp
from jax import lax
from jax.experimental import pallas as pl
from jax.experimental.pallas import tpu as pltpu
from jax.sharding import PartitionSpec as P


EXTRA = 8
PARTS = 3
GRANT = 4 << 20
MESSAGES = ((4, (0,)), (2, (0,)), (1, (0,)), (2, (4,)), (1, (2,)), (1, (4,)), (1, (6,)))


def centered(values, mean, factor):
    return ((values.astype(jnp.float32) - mean) * factor).astype(jnp.bfloat16)


def parts_of(value):
    parts = []
    for _ in range(PARTS):
        part = value.astype(jnp.bfloat16).astype(jnp.float32)
        value = value - part
        parts.append(part)
    return parts


def call(kernel, out_shape, scratch=()):
    return pl.pallas_call(
        kernel,
        out_shape=out_shape,
        scratch_shapes=scratch,
        compiler_params=pltpu.CompilerParams(vmem_limit_bytes=GRANT),
    )


def pack_kernel(values_hbm, epsilon_hbm, packed_ref, values, epsilon, arrived):
    rows, columns = values.shape
    copies = [
        pltpu.make_async_copy(source, target, arrived.at[at])
        for at, (source, target) in enumerate(((values_hbm, values), (epsilon_hbm, epsilon)))
    ]
    for copy in copies:
        copy.start()
    for copy in copies:
        copy.wait()
    block = values[...]
    packed_ref[:rows, :] = block
    wide = [jnp.zeros((1, columns - rows), jnp.float32)]
    lines = [jnp.concatenate([part] + wide, axis=1) for part in parts_of(epsilon[...])]
    lines += parts_of(jnp.sum(block.astype(jnp.float32), axis=0, keepdims=True))
    lines.append(jnp.zeros((EXTRA - 2 * PARTS, columns), jnp.float32))
    packed_ref[rows:, :] = jnp.concatenate(lines, axis=0).astype(jnp.bfloat16)


def pack(derivatives, epsilon):
    rows, columns = derivatives.shape
    return pl.pallas_call(
        pack_kernel,
        out_shape=jax.ShapeDtypeStruct((rows + EXTRA, columns), jnp.bfloat16),
        in_specs=[pl.BlockSpec(memory_space=pltpu.HBM)] * 2,
        scratch_shapes=[pltpu.VMEM((rows, columns), jnp.bfloat16), pltpu.VMEM((1, rows), jnp.float32), pltpu.SemaphoreType.DMA((2,))],
        compiler_params=pltpu.CompilerParams(vmem_limit_bytes=GRANT),
        name="pack",
    )(pltpu.with_memory_space_constraint(derivatives, pltpu.HBM), pltpu.with_memory_space_constraint(epsilon.reshape(1, rows), pltpu.HBM))


def join_kernel(packed, places, *refs):
    arrays, joined_ref = refs[:-1], refs[-1]
    for slot, (at, place) in enumerate(places):
        joined_ref[slot * packed : (slot + 1) * packed, :] = arrays[at][place * packed : (place + 1) * packed, :]


def tile_kernel(total_rows, where, *refs):
    count = 1 + max(at for at, _ in where)
    arrays, (kept_ref, sent_ref, update_ref, held, lines) = refs[:count], refs[count:]
    n, _ = lines.shape
    rows = total_rows // n
    packed = rows + EXTRA
    me, mine = lax.axis_index("smp"), lax.axis_index("par")
    factor = 1.0 / math.sqrt(total_rows)
    blocks = [arrays[at].at[packed * slot : packed * (slot + 1), :] for at, slot in where]
    for step, block in enumerate(blocks):
        tail = block[rows:, :].astype(jnp.float32)
        lines[pl.ds(jnp.bitwise_xor(me, step), 1), :] = jnp.sum(tail[PARTS : 2 * PARTS, :], axis=0, keepdims=True)
    mean = jnp.sum(lines[...], axis=0, keepdims=True) / total_rows
    own = None
    for step, block in enumerate(blocks):
        terms = centered(block[:rows, :], mean, factor)
        own = terms if step == 0 else own
        source = jnp.bitwise_xor(me, step)
        place = jnp.bitwise_xor(source // 2, mine) * 2 + source % 2
        held[pl.ds(pl.multiple_of(place * rows, rows), rows), :] = terms
        weighted = jnp.dot(block[rows:, :rows], terms, preferred_element_type=jnp.float32)
        lines[pl.ds(source, 1), :] = jnp.sum(weighted[:PARTS, :], axis=0, keepdims=True)
    half = total_rows // 2
    contract = (((1,), (1,)), ((), ()))
    sent_ref[...] = lax.dot_general(own, held[half:, :], contract, preferred_element_type=jnp.float32).astype(jnp.bfloat16)
    kept_ref[...] = lax.dot_general(own, held[:half, :], contract, preferred_element_type=jnp.float32)
    update_ref[...] = jnp.sum(lines[...], axis=0, keepdims=True)


def swap(value, axis, bit):
    return lax.ppermute(value, axis, [(i, i ^ bit) for i in range(lax.axis_size(axis))])


def direct(derivatives, epsilon):
    n, m = lax.axis_size("smp"), lax.axis_size("par")
    rows, columns = derivatives.shape
    half = rows * n // 2
    height = rows + EXTRA
    arrays, where = [pack(derivatives, epsilon)], {0: (0, 0)}
    for at, (bit, sources) in enumerate(MESSAGES):
        used = sorted({where[source][0] for source in sources})
        value = arrays[used[0]]
        if len(used) > 1 or value.shape[0] != len(sources) * height:
            places = tuple((used.index(where[source][0]), where[source][1]) for source in sources)
            shape = jax.ShapeDtypeStruct((len(sources) * height, columns), jnp.bfloat16)
            value = call(functools.partial(join_kernel, height, places), shape)(*(arrays[one] for one in used))
        arrays.append(swap(value, "smp", bit))
        for slot, source in enumerate(sources):
            where[source ^ bit] = (at + 1, slot)
    kept, sent, update = call(
        functools.partial(tile_kernel, rows * n, tuple(where[step] for step in range(n))),
        (
            jax.ShapeDtypeStruct((rows, half), jnp.float32),
            jax.ShapeDtypeStruct((rows, half), jnp.bfloat16),
            jax.ShapeDtypeStruct((1, columns), jnp.float32),
        ),
        [pltpu.VMEM((n * rows, columns), jnp.bfloat16), pltpu.VMEM((n, columns), jnp.float32)],
    )(*arrays)
    both = kept + swap(sent, "par", 2).astype(jnp.float32)
    width = rows * n // m
    gram_tile = both[:, :width] + swap(both[:, width:], "par", 1)
    return (gram_tile, update.reshape(-1))


def gathered(derivatives, epsilon):
    total_rows = derivatives.shape[0] * lax.axis_size("smp")
    factor = 1.0 / math.sqrt(total_rows)
    everything = lax.all_gather(derivatives, "smp", axis=0, tiled=True)
    mean = jnp.sum(everything.astype(jnp.float32), axis=0) / total_rows
    own = centered(derivatives, mean, factor)
    partial_terms = jnp.dot(own, centered(everything, mean, factor).T, preferred_element_type=jnp.float32)
    gram_tile = lax.psum_scatter(partial_terms, "par", scatter_dimension=1, tiled=True)
    local_sum = jnp.dot(epsilon, own.astype(jnp.float32), precision=lax.Precision.HIGHEST)
    return (gram_tile, lax.psum(local_sum, "smp"))


def solution(mesh):
    in_specs = (P("smp", "par"), P("smp"))
    out_specs = (P("smp", "par"), P("par"))

    def shards(derivatives, epsilon):
        return (direct if small else gathered)(derivatives, epsilon)

    small = (mesh.shape["smp"], mesh.shape["par"]) == (8, 4)
    return jax.shard_map(shards, mesh=mesh, in_specs=in_specs, out_specs=out_specs, check_vma=False)
```

```python
import functools
import math

import jax
import jax.numpy as jnp
from jax import lax
from jax.experimental import pallas as pl
from jax.experimental.pallas import tpu as pltpu
from jax.sharding import PartitionSpec as P


EXTRA = 8
PARTS = 3
GRANT = 4 << 20
MESSAGES = ((4, (0,)), (2, (0,)), (1, (0,)), (2, (4,)), (1, (2,)), (1, (4,)), (1, (6,)))


def centered(values, mean, factor):
    return ((values.astype(jnp.float32) - mean) * factor).astype(jnp.bfloat16)


def parts_of(value):
    parts = []
    for _ in range(PARTS):
        part = value.astype(jnp.bfloat16).astype(jnp.float32)
        value = value - part
        parts.append(part)
    return parts


def call(kernel, out_shape, scratch=()):
    return pl.pallas_call(
        kernel,
        out_shape=out_shape,
        scratch_shapes=scratch,
        compiler_params=pltpu.CompilerParams(vmem_limit_bytes=GRANT),
    )


def pack_kernel(values_hbm, epsilon_hbm, packed_ref, values, epsilon, arrived):
    rows, columns = values.shape
    copies = [
        pltpu.make_async_copy(source, target, arrived.at[at])
        for at, (source, target) in enumerate(((values_hbm, values), (epsilon_hbm, epsilon)))
    ]
    for copy in copies:
        copy.start()
    for copy in copies:
        copy.wait()
    block = values[...]
    packed_ref[:rows, :] = block
    wide = [jnp.zeros((1, columns - rows), jnp.float32)]
    lines = [jnp.concatenate([part] + wide, axis=1) for part in parts_of(epsilon[...])]
    lines += parts_of(jnp.sum(block.astype(jnp.float32), axis=0, keepdims=True))
    lines.append(jnp.zeros((EXTRA - 2 * PARTS, columns), jnp.float32))
    packed_ref[rows:, :] = jnp.concatenate(lines, axis=0).astype(jnp.bfloat16)


def pack(derivatives, epsilon):
    rows, columns = derivatives.shape
    return pl.pallas_call(
        pack_kernel,
        out_shape=jax.ShapeDtypeStruct((rows + EXTRA, columns), jnp.bfloat16),
        in_specs=[pl.BlockSpec(memory_space=pltpu.HBM)] * 2,
        scratch_shapes=[pltpu.VMEM((rows, columns), jnp.bfloat16), pltpu.VMEM((1, rows), jnp.float32), pltpu.SemaphoreType.DMA((2,))],
        compiler_params=pltpu.CompilerParams(vmem_limit_bytes=GRANT),
        name="pack",
    )(pltpu.with_memory_space_constraint(derivatives, pltpu.HBM), pltpu.with_memory_space_constraint(epsilon.reshape(1, rows), pltpu.HBM))


def join_kernel(packed, places, *refs):
    arrays, joined_ref = refs[:-1], refs[-1]
    for slot, (at, place) in enumerate(places):
        joined_ref[slot * packed : (slot + 1) * packed, :] = arrays[at][place * packed : (place + 1) * packed, :]


def source_of(step):
    return jnp.bitwise_xor(lax.axis_index("smp"), step)


def place_of(step, rows):
    source = source_of(step)
    apart = jnp.bitwise_xor(source // 2, lax.axis_index("par"))
    place = apart % 2 * 4 + apart // 2 * 2 + source % 2
    return pl.ds(pl.multiple_of(place * rows, rows), rows)


def product(left, right):
    return lax.dot_general(left, right, (((1,), (1,)), ((), ())), preferred_element_type=jnp.float32)


def blocks_of(where, arrays, packed):
    return [arrays[at].at[packed * slot : packed * (slot + 1), :] for at, slot in where]


def send_kernel(total_rows, where, *refs):
    arrays, (sent_ref, held_ref, lines) = refs[:-3], refs[-3:]
    rows = total_rows // len(where)
    factor = 1.0 / math.sqrt(total_rows)
    blocks = blocks_of(where, arrays, rows + EXTRA)
    for step, block in enumerate(blocks):
        tail = block[rows:, :].astype(jnp.float32)
        lines[pl.ds(source_of(step), 1), :] = jnp.sum(tail[PARTS : 2 * PARTS, :], axis=0, keepdims=True)
    mean = jnp.sum(lines[...], axis=0, keepdims=True) / total_rows
    own = None
    for step, block in enumerate(blocks):
        terms = centered(block[:rows, :], mean, factor)
        own = terms if step == 0 else own
        held_ref[place_of(step, rows), :] = terms
    for slot in range(2):
        sent_ref[slot] = product(own, held_ref[(slot + 2) * total_rows // 4 : (slot + 3) * total_rows // 4, :])


def keep_kernel(total_rows, where, held_ref, *refs):
    arrays, (kept_ref, update_ref, lines) = refs[:-3], refs[-3:]
    rows = total_rows // len(where)
    for step, block in enumerate(blocks_of(where, arrays, rows + EXTRA)):
        terms = held_ref[place_of(step, rows), :]
        weighted = jnp.dot(block[rows:, :rows], terms, preferred_element_type=jnp.float32)
        lines[pl.ds(source_of(step), 1), :] = jnp.sum(weighted[:PARTS, :], axis=0, keepdims=True)
    update_ref[...] = jnp.sum(lines[...], axis=0, keepdims=True)
    own = held_ref[place_of(0, rows), :]
    for slot in range(2):
        kept_ref[slot] = product(own, held_ref[slot * total_rows // 4 : (slot + 1) * total_rows // 4, :])


def swap(value, axis, bit):
    return lax.ppermute(value, axis, [(i, i ^ bit) for i in range(lax.axis_size(axis))])


def direct(derivatives, epsilon):
    n, m = lax.axis_size("smp"), lax.axis_size("par")
    rows, columns = derivatives.shape
    height = rows + EXTRA
    arrays, where = [pack(derivatives, epsilon)], {0: (0, 0)}
    for at, (bit, sources) in enumerate(MESSAGES):
        used = sorted({where[source][0] for source in sources})
        value = arrays[used[0]]
        if len(used) > 1 or value.shape[0] != len(sources) * height:
            places = tuple((used.index(where[source][0]), where[source][1]) for source in sources)
            shape = jax.ShapeDtypeStruct((len(sources) * height, columns), jnp.bfloat16)
            value = call(functools.partial(join_kernel, height, places), shape)(*(arrays[one] for one in used))
        arrays.append(swap(value, "smp", bit))
        for slot, source in enumerate(sources):
            where[source ^ bit] = (at + 1, slot)
    where = tuple(where[step] for step in range(n))
    lines = [pltpu.VMEM((n, columns), jnp.float32)]
    tile = jax.ShapeDtypeStruct((2, rows, rows * n // m), jnp.float32)
    sent, held = call(
        functools.partial(send_kernel, rows * n, where),
        (tile, jax.ShapeDtypeStruct((n * rows, columns), jnp.bfloat16)),
        lines,
    )(*arrays)
    got = swap(sent, "par", 1)
    kept, update = call(
        functools.partial(keep_kernel, rows * n, where), (tile, jax.ShapeDtypeStruct((1, columns), jnp.float32)), lines
    )(held, *arrays)
    both = kept + got
    gram_tile = both[0] + swap(both[1].astype(jnp.bfloat16), "par", 2).astype(jnp.float32)
    return (gram_tile, update.reshape(-1))


def gathered(derivatives, epsilon):
    total_rows = derivatives.shape[0] * lax.axis_size("smp")
    factor = 1.0 / math.sqrt(total_rows)
    everything = lax.all_gather(derivatives, "smp", axis=0, tiled=True)
    mean = jnp.sum(everything.astype(jnp.float32), axis=0) / total_rows
    own = centered(derivatives, mean, factor)
    partial_terms = jnp.dot(own, centered(everything, mean, factor).T, preferred_element_type=jnp.float32)
    gram_tile = lax.psum_scatter(partial_terms, "par", scatter_dimension=1, tiled=True)
    local_sum = jnp.dot(epsilon, own.astype(jnp.float32), precision=lax.Precision.HIGHEST)
    return (gram_tile, lax.psum(local_sum, "smp"))


def solution(mesh):
    in_specs = (P("smp", "par"), P("smp"))
    out_specs = (P("smp", "par"), P("par"))

    def shards(derivatives, epsilon):
        return (direct if small else gathered)(derivatives, epsilon)

    small = (mesh.shape["smp"], mesh.shape["par"]) == (8, 4)
    return jax.shard_map(shards, mesh=mesh, in_specs=in_specs, out_specs=out_specs, check_vma=False)
```

```python
import functools
import math

import jax
import jax.numpy as jnp
from jax import lax
from jax.experimental import pallas as pl
from jax.experimental.pallas import tpu as pltpu
from jax.sharding import PartitionSpec as P


EXTRA = 8
PARTS = 3
GRANT = 4 << 20
LANES = 128
SPARE = 8


def centered(values, mean, factor):
    return ((values.astype(jnp.float32) - mean) * factor).astype(jnp.bfloat16)


def parts_of(value):
    parts = []
    for _ in range(PARTS):
        part = value.astype(jnp.bfloat16).astype(jnp.float32)
        value = value - part
        parts.append(part)
    return parts


def call(kernel, out_shape, scratch=()):
    return pl.pallas_call(
        kernel,
        out_shape=out_shape,
        scratch_shapes=scratch,
        compiler_params=pltpu.CompilerParams(vmem_limit_bytes=GRANT),
    )


def pack_kernel(values_hbm, epsilon_hbm, packed_ref, values, epsilon, arrived):
    rows, columns = values.shape
    copies = [
        pltpu.make_async_copy(source, target, arrived.at[at])
        for at, (source, target) in enumerate(((values_hbm, values), (epsilon_hbm, epsilon)))
    ]
    for copy in copies:
        copy.start()
    for copy in copies:
        copy.wait()
    block = values[...]
    packed_ref[:rows, :] = block
    wide = [jnp.zeros((1, columns - rows), jnp.float32)]
    lines = [jnp.concatenate([part] + wide, axis=1) for part in parts_of(epsilon[...])]
    lines += parts_of(jnp.sum(block.astype(jnp.float32), axis=0, keepdims=True))
    lines.append(jnp.zeros((EXTRA - 2 * PARTS, columns), jnp.float32))
    packed_ref[rows:, :] = jnp.concatenate(lines, axis=0).astype(jnp.bfloat16)


def pack(derivatives, epsilon):
    rows, columns = derivatives.shape
    return pl.pallas_call(
        pack_kernel,
        out_shape=jax.ShapeDtypeStruct((rows + EXTRA, columns), jnp.bfloat16),
        in_specs=[pl.BlockSpec(memory_space=pltpu.HBM)] * 2,
        scratch_shapes=[pltpu.VMEM((rows, columns), jnp.bfloat16), pltpu.VMEM((1, rows), jnp.float32), pltpu.SemaphoreType.DMA((2,))],
        compiler_params=pltpu.CompilerParams(vmem_limit_bytes=GRANT),
        name="pack",
    )(pltpu.with_memory_space_constraint(derivatives, pltpu.HBM), pltpu.with_memory_space_constraint(epsilon.reshape(1, rows), pltpu.HBM))


def tails_kernel(*refs):
    for slot, ref in enumerate(refs[:-1]):
        tail = ref[ref.shape[0] - EXTRA :, : refs[-1].shape[1]]
        refs[-1][slot * EXTRA : (slot + 1) * EXTRA, :] = tail


def source_of(step):
    return jnp.bitwise_xor(lax.axis_index("smp"), step)


def place_of(step, rows):
    source = source_of(step)
    apart = jnp.bitwise_xor(source // 2, lax.axis_index("par"))
    place = apart % 2 * 4 + apart // 2 * 2 + source % 2
    return pl.ds(pl.multiple_of(place * rows, rows), rows)


def product(left, right):
    return lax.dot_general(left, right, (((1,), (1,)), ((), ())), preferred_element_type=jnp.float32)


def send_kernel(total_rows, *refs):
    blocks, (sent_ref, held_ref, lines) = refs[:-3], refs[-3:]
    rows = total_rows // len(blocks)
    factor = 1.0 / math.sqrt(total_rows)
    for step, block in enumerate(blocks):
        if block.shape[0] > rows:
            line = jnp.sum(block[rows:, :].astype(jnp.float32)[PARTS : 2 * PARTS, :], axis=0, keepdims=True)
        else:
            line = jnp.sum(block[...].astype(jnp.float32), axis=0, keepdims=True)
        lines[pl.ds(source_of(step), 1), :] = line
    mean = jnp.sum(lines[: len(blocks), :], axis=0, keepdims=True) / total_rows
    own = None
    for step, block in enumerate(blocks):
        terms = centered(block[:rows, :], mean, factor)
        own = terms if step == 0 else own
        held_ref[place_of(step, rows), :] = terms
    for slot in range(2):
        sent_ref[slot] = product(own, held_ref[(slot + 2) * total_rows // 4 : (slot + 3) * total_rows // 4, :])


def keep_kernel(rows, held_ref, kept_ref):
    own = held_ref[place_of(0, rows), :]
    for slot in range(2):
        span = held_ref.shape[0] // 4
        kept_ref[slot] = product(own, held_ref[slot * span : (slot + 1) * span, :])


def update_kernel(rows, held_ref, near_ref, far_ref, update_ref, lines):
    count = held_ref.shape[0] // rows
    for step in range(count):
        ref, slot = (near_ref, step) if step < 4 else (far_ref, step - 4)
        weights = ref[slot * EXTRA : (slot + 1) * EXTRA, :rows]
        weighted = jnp.dot(weights, held_ref[place_of(step, rows), :], preferred_element_type=jnp.float32)
        lines[pl.ds(source_of(step), 1), :] = jnp.sum(weighted[:PARTS, :], axis=0, keepdims=True)
    update_ref[...] = jnp.sum(lines[:count, :], axis=0, keepdims=True)


def swap(value, axis, bit):
    return lax.ppermute(value, axis, [(i, i ^ bit) for i in range(lax.axis_size(axis))])


def direct(derivatives, epsilon):
    n, m = lax.axis_size("smp"), lax.axis_size("par")
    rows, columns = derivatives.shape
    far = swap(derivatives, "smp", 4)
    own = pack(derivatives, epsilon)
    beside = swap(own, "smp", 2)
    other = swap(own, "smp", 1)
    far_beside = swap(far, "smp", 2)
    beside_other = swap(other, "smp", 2)
    far_other = swap(far, "smp", 1)
    far_beside_other = swap(far_beside, "smp", 1)
    near = (own, other, beside, beside_other)
    tails = call(tails_kernel, jax.ShapeDtypeStruct((len(near) * EXTRA, LANES), jnp.bfloat16))(*near)
    far_tails = swap(tails, "smp", 4)
    tile = jax.ShapeDtypeStruct((2, rows, rows * n // m), jnp.float32)
    lines = [pltpu.VMEM((n + SPARE, columns), jnp.float32)]
    sent, held = call(
        functools.partial(send_kernel, rows * n), (tile, jax.ShapeDtypeStruct((n * rows, columns), jnp.bfloat16)), lines
    )(*near, far, far_other, far_beside, far_beside_other)
    got = swap(sent, "par", 1)
    kept = call(functools.partial(keep_kernel, rows), tile)(held)
    line = jax.ShapeDtypeStruct((1, columns), jnp.float32)
    update = call(functools.partial(update_kernel, rows), line, lines)(held, tails, far_tails)
    both = kept + got
    gram_tile = both[0] + swap(both[1].astype(jnp.bfloat16), "par", 2).astype(jnp.float32)
    return (gram_tile, update.reshape(-1))


def gathered(derivatives, epsilon):
    total_rows = derivatives.shape[0] * lax.axis_size("smp")
    factor = 1.0 / math.sqrt(total_rows)
    everything = lax.all_gather(derivatives, "smp", axis=0, tiled=True)
    mean = jnp.sum(everything.astype(jnp.float32), axis=0) / total_rows
    own = centered(derivatives, mean, factor)
    partial_terms = jnp.dot(own, centered(everything, mean, factor).T, preferred_element_type=jnp.float32)
    gram_tile = lax.psum_scatter(partial_terms, "par", scatter_dimension=1, tiled=True)
    local_sum = jnp.dot(epsilon, own.astype(jnp.float32), precision=lax.Precision.HIGHEST)
    return (gram_tile, lax.psum(local_sum, "smp"))


def solution(mesh):
    in_specs = (P("smp", "par"), P("smp"))
    out_specs = (P("smp", "par"), P("par"))

    def shards(derivatives, epsilon):
        return (direct if small else gathered)(derivatives, epsilon)

    small = (mesh.shape["smp"], mesh.shape["par"]) == (8, 4)
    return jax.shard_map(shards, mesh=mesh, in_specs=in_specs, out_specs=out_specs, check_vma=False)
```

```python
import functools
import math

import jax
import jax.numpy as jnp
from jax import lax
from jax.experimental import pallas as pl
from jax.experimental.pallas import tpu as pltpu
from jax.sharding import PartitionSpec as P


EXTRA = 8
PARTS = 3
GRANT = 4 << 20
LANES = 128
GROUP = 24
SPARE = 8


def centered(values, mean, factor):
    return ((values.astype(jnp.float32) - mean) * factor).astype(jnp.bfloat16)


def parts_of(value):
    parts = []
    for _ in range(PARTS):
        part = value.astype(jnp.bfloat16).astype(jnp.float32)
        value = value - part
        parts.append(part)
    return parts


def call(kernel, out_shape, scratch=()):
    return pl.pallas_call(
        kernel,
        out_shape=out_shape,
        scratch_shapes=scratch,
        compiler_params=pltpu.CompilerParams(vmem_limit_bytes=GRANT),
    )


def pack_kernel(values_hbm, epsilon_hbm, packed_ref, values, epsilon, arrived):
    rows, columns = values.shape
    copies = [
        pltpu.make_async_copy(source, target, arrived.at[at])
        for at, (source, target) in enumerate(((values_hbm, values), (epsilon_hbm, epsilon)))
    ]
    for copy in copies:
        copy.start()
    for copy in copies:
        copy.wait()
    block = values[...]
    packed_ref[:rows, :] = block
    wide = [jnp.zeros((1, columns - rows), jnp.float32)]
    lines = [jnp.concatenate([part] + wide, axis=1) for part in parts_of(epsilon[...])]
    lines += parts_of(jnp.sum(block.astype(jnp.float32), axis=0, keepdims=True))
    lines.append(jnp.zeros((EXTRA - 2 * PARTS, columns), jnp.float32))
    packed_ref[rows:, :] = jnp.concatenate(lines, axis=0).astype(jnp.bfloat16)


def pack(derivatives, epsilon):
    rows, columns = derivatives.shape
    return pl.pallas_call(
        pack_kernel,
        out_shape=jax.ShapeDtypeStruct((rows + EXTRA, columns), jnp.bfloat16),
        in_specs=[pl.BlockSpec(memory_space=pltpu.HBM)] * 2,
        scratch_shapes=[pltpu.VMEM((rows, columns), jnp.bfloat16), pltpu.VMEM((1, rows), jnp.float32), pltpu.SemaphoreType.DMA((2,))],
        compiler_params=pltpu.CompilerParams(vmem_limit_bytes=GRANT),
        name="pack",
    )(pltpu.with_memory_space_constraint(derivatives, pltpu.HBM), pltpu.with_memory_space_constraint(epsilon.reshape(1, rows), pltpu.HBM))


def tails_kernel(*refs):
    for slot, ref in enumerate(refs[:-1]):
        tail = ref[ref.shape[0] - EXTRA :, : refs[-1].shape[1]]
        refs[-1][slot * EXTRA : (slot + 1) * EXTRA, :] = tail


def source_of(step):
    return jnp.bitwise_xor(lax.axis_index("smp"), step)


def place_of(step, rows):
    source = source_of(step)
    apart = jnp.bitwise_xor(source // 2, lax.axis_index("par"))
    place = apart % 2 * 4 + apart // 2 * 2 + source % 2
    return pl.ds(pl.multiple_of(place * rows, rows), rows)


def product(left, right):
    return lax.dot_general(left, right, (((1,), (1,)), ((), ())), preferred_element_type=jnp.float32)


def send_kernel(total_rows, *refs):
    blocks, (sent_ref, held_ref, lines) = refs[:-3], refs[-3:]
    rows = total_rows // len(blocks)
    factor = 1.0 / math.sqrt(total_rows)
    for step, block in enumerate(blocks):
        if block.shape[0] > rows:
            line = jnp.sum(block[rows:, :].astype(jnp.float32)[PARTS : 2 * PARTS, :], axis=0, keepdims=True)
        else:
            line = jnp.sum(block[...].astype(jnp.float32), axis=0, keepdims=True)
        lines[pl.ds(source_of(step), 1), :] = line
    mean = jnp.sum(lines[: len(blocks), :], axis=0, keepdims=True) / total_rows
    own = None
    for step, block in enumerate(blocks):
        terms = centered(block[:rows, :], mean, factor)
        own = terms if step == 0 else own
        held_ref[place_of(step, rows), :] = terms
    for slot in range(2):
        sent_ref[slot] = product(own, held_ref[(slot + 2) * total_rows // 4 : (slot + 3) * total_rows // 4, :])


def keep_kernel(rows, held_ref, kept_ref):
    own = held_ref[place_of(0, rows), :]
    for slot in range(2):
        span = held_ref.shape[0] // 4
        kept_ref[slot] = product(own, held_ref[slot * span : (slot + 1) * span, :])


def update_kernel(rows, held_ref, near_ref, far_ref, update_ref, lines):
    count = held_ref.shape[0] // rows
    for step in range(count):
        ref, slot = (near_ref, step) if step < 4 else (far_ref, step - 4)
        weights = ref[slot * EXTRA : (slot + 1) * EXTRA, :rows]
        weighted = jnp.dot(weights, held_ref[place_of(step, rows), :], preferred_element_type=jnp.float32)
        lines[pl.ds(source_of(step), 1), :] = jnp.sum(weighted[:PARTS, :], axis=0, keepdims=True)
    update_ref[...] = jnp.sum(lines[:count, :], axis=0, keepdims=True)


def middle_kernel(kept_ref, got_ref, base_ref, packed_ref):
    base_ref[...] = kept_ref[0] + got_ref[0]
    tile = kept_ref[1] + got_ref[1]
    rows, width = tile.shape
    packed_ref[:rows, :] = tile[:, :LANES].astype(jnp.bfloat16)
    rest = jnp.concatenate([tile[:, LANES:], jnp.zeros((4 * GROUP - rows, width - LANES), jnp.float32)], axis=0)
    pieces = [rest[at * GROUP : (at + 1) * GROUP, :] for at in range(4)]
    packed_ref[rows:, :] = jnp.concatenate(pieces, axis=1).astype(jnp.bfloat16)


def last_kernel(base_ref, packed_ref, tile_ref):
    rows, width = base_ref.shape
    side = width - LANES
    tile_ref[:, :LANES] = base_ref[:, :LANES] + packed_ref[:rows, :].astype(jnp.float32)
    rest = packed_ref[rows:, :].astype(jnp.float32)
    pieces = [rest[:, at * side : (at + 1) * side] for at in range(4)]
    tile_ref[:, LANES:] = base_ref[:, LANES:] + jnp.concatenate(pieces, axis=0)[:rows, :]


def swap(value, axis, bit):
    return lax.ppermute(value, axis, [(i, i ^ bit) for i in range(lax.axis_size(axis))])


def direct(derivatives, epsilon):
    n, m = lax.axis_size("smp"), lax.axis_size("par")
    rows, columns = derivatives.shape
    far = swap(derivatives, "smp", 4)
    own = pack(derivatives, epsilon)
    beside = swap(own, "smp", 2)
    other = swap(own, "smp", 1)
    far_beside = swap(far, "smp", 2)
    beside_other = swap(other, "smp", 2)
    far_other = swap(far, "smp", 1)
    far_beside_other = swap(far_beside, "smp", 1)
    near = (own, other, beside, beside_other)
    tails = call(tails_kernel, jax.ShapeDtypeStruct((len(near) * EXTRA, LANES), jnp.bfloat16))(*near)
    far_tails = swap(tails, "smp", 4)
    tile = jax.ShapeDtypeStruct((2, rows, rows * n // m), jnp.float32)
    lines = [pltpu.VMEM((n + SPARE, columns), jnp.float32)]
    sent, held = call(
        functools.partial(send_kernel, rows * n), (tile, jax.ShapeDtypeStruct((n * rows, columns), jnp.bfloat16)), lines
    )(*near, far, far_other, far_beside, far_beside_other)
    got = swap(sent, "par", 1)
    kept = call(functools.partial(keep_kernel, rows), tile)(held)
    line = jax.ShapeDtypeStruct((1, columns), jnp.float32)
    update = call(functools.partial(update_kernel, rows), line, lines)(held, tails, far_tails)
    packed_rows = rows + GROUP
    base, packed = call(
        middle_kernel,
        (jax.ShapeDtypeStruct(tile.shape[1:], jnp.float32), jax.ShapeDtypeStruct((packed_rows, LANES), jnp.bfloat16)),
    )(kept, got)
    gram_tile = call(last_kernel, jax.ShapeDtypeStruct(tile.shape[1:], jnp.float32))(base, swap(packed, "par", 2))
    return (gram_tile, update.reshape(-1))


def gathered(derivatives, epsilon):
    total_rows = derivatives.shape[0] * lax.axis_size("smp")
    factor = 1.0 / math.sqrt(total_rows)
    everything = lax.all_gather(derivatives, "smp", axis=0, tiled=True)
    mean = jnp.sum(everything.astype(jnp.float32), axis=0) / total_rows
    own = centered(derivatives, mean, factor)
    partial_terms = jnp.dot(own, centered(everything, mean, factor).T, preferred_element_type=jnp.float32)
    gram_tile = lax.psum_scatter(partial_terms, "par", scatter_dimension=1, tiled=True)
    local_sum = jnp.dot(epsilon, own.astype(jnp.float32), precision=lax.Precision.HIGHEST)
    return (gram_tile, lax.psum(local_sum, "smp"))


def solution(mesh):
    in_specs = (P("smp", "par"), P("smp"))
    out_specs = (P("smp", "par"), P("par"))

    def shards(derivatives, epsilon):
        return (direct if small else gathered)(derivatives, epsilon)

    small = (mesh.shape["smp"], mesh.shape["par"]) == (8, 4)
    return jax.shard_map(shards, mesh=mesh, in_specs=in_specs, out_specs=out_specs, check_vma=False)
```

```python
import functools
import math

import jax
import jax.numpy as jnp
from jax import lax
from jax.experimental import pallas as pl
from jax.experimental.pallas import tpu as pltpu
from jax.sharding import PartitionSpec as P


EXTRA = 8
PARTS = 3
GRANT = 4 << 20
LANES = 128
GROUP = 24
SPARE = 8


def centered(values, mean, factor):
    return ((values.astype(jnp.float32) - mean) * factor).astype(jnp.bfloat16)


def parts_of(value):
    parts = []
    for _ in range(PARTS):
        part = value.astype(jnp.bfloat16).astype(jnp.float32)
        value = value - part
        parts.append(part)
    return parts


def call(kernel, out_shape, scratch=()):
    return pl.pallas_call(
        kernel,
        out_shape=out_shape,
        scratch_shapes=scratch,
        compiler_params=pltpu.CompilerParams(vmem_limit_bytes=GRANT),
    )


def pack_kernel(values_hbm, epsilon_hbm, packed_ref, values, epsilon, arrived):
    rows, columns = values.shape
    copies = [
        pltpu.make_async_copy(source, target, arrived.at[at])
        for at, (source, target) in enumerate(((values_hbm, values), (epsilon_hbm, epsilon)))
    ]
    for copy in copies:
        copy.start()
    for copy in copies:
        copy.wait()
    block = values[...]
    packed_ref[:rows, :] = block
    wide = [jnp.zeros((1, columns - rows), jnp.float32)]
    lines = [jnp.concatenate([part] + wide, axis=1) for part in parts_of(epsilon[...])]
    lines += parts_of(jnp.sum(block.astype(jnp.float32), axis=0, keepdims=True))
    lines.append(jnp.zeros((EXTRA - 2 * PARTS, columns), jnp.float32))
    packed_ref[rows:, :] = jnp.concatenate(lines, axis=0).astype(jnp.bfloat16)


def pack(derivatives, epsilon):
    rows, columns = derivatives.shape
    return pl.pallas_call(
        pack_kernel,
        out_shape=jax.ShapeDtypeStruct((rows + EXTRA, columns), jnp.bfloat16),
        in_specs=[pl.BlockSpec(memory_space=pltpu.HBM)] * 2,
        scratch_shapes=[pltpu.VMEM((rows, columns), jnp.bfloat16), pltpu.VMEM((1, rows), jnp.float32), pltpu.SemaphoreType.DMA((2,))],
        compiler_params=pltpu.CompilerParams(vmem_limit_bytes=GRANT),
        name="pack",
    )(pltpu.with_memory_space_constraint(derivatives, pltpu.HBM), pltpu.with_memory_space_constraint(epsilon.reshape(1, rows), pltpu.HBM))


def tails_kernel(*refs):
    packed, raw, (tails_ref, sums_ref) = refs[:4], refs[4:-2], refs[-2:]
    for slot, ref in enumerate(packed):
        tails_ref[slot * EXTRA : (slot + 1) * EXTRA, :] = ref[ref.shape[0] - EXTRA :, : tails_ref.shape[1]]
    for slot, ref in enumerate(raw):
        sums_ref[slot : slot + 1, :] = jnp.sum(ref[...].astype(jnp.float32), axis=0, keepdims=True)


def source_of(step):
    return jnp.bitwise_xor(lax.axis_index("smp"), step)


def place_of(step, rows):
    source = source_of(step)
    apart = jnp.bitwise_xor(source // 2, lax.axis_index("par"))
    place = apart % 2 * 4 + apart // 2 * 2 + source % 2
    return pl.ds(pl.multiple_of(place * rows, rows), rows)


def product(left, right):
    return lax.dot_general(left, right, (((1,), (1,)), ((), ())), preferred_element_type=jnp.float32)


def send_kernel(total_rows, early, sums_ref, *refs):
    blocks, (sent_ref, held_ref, lines) = refs[:-3], refs[-3:]
    rows = total_rows // len(blocks)
    factor = 1.0 / math.sqrt(total_rows)
    for step, block in enumerate(blocks):
        if block.shape[0] > rows:
            line = jnp.sum(block[rows:, :].astype(jnp.float32)[PARTS : 2 * PARTS, :], axis=0, keepdims=True)
        elif step in early:
            line = sums_ref[early.index(step) : early.index(step) + 1, :]
        else:
            line = jnp.sum(block[...].astype(jnp.float32), axis=0, keepdims=True)
        lines[pl.ds(source_of(step), 1), :] = line
    mean = jnp.sum(lines[: len(blocks), :], axis=0, keepdims=True) / total_rows
    own = None
    for step, block in enumerate(blocks):
        terms = centered(block[:rows, :], mean, factor)
        own = terms if step == 0 else own
        held_ref[place_of(step, rows), :] = terms
    for slot in range(2):
        sent_ref[slot] = product(own, held_ref[(slot + 2) * total_rows // 4 : (slot + 3) * total_rows // 4, :])


def keep_kernel(rows, held_ref, kept_ref):
    own = held_ref[place_of(0, rows), :]
    for slot in range(2):
        span = held_ref.shape[0] // 4
        kept_ref[slot] = product(own, held_ref[slot * span : (slot + 1) * span, :])


def update_kernel(rows, held_ref, near_ref, far_ref, update_ref, lines):
    count = held_ref.shape[0] // rows
    for step in range(count):
        ref, slot = (near_ref, step) if step < 4 else (far_ref, step - 4)
        weights = ref[slot * EXTRA : (slot + 1) * EXTRA, :rows]
        weighted = jnp.dot(weights, held_ref[place_of(step, rows), :], preferred_element_type=jnp.float32)
        lines[pl.ds(source_of(step), 1), :] = jnp.sum(weighted[:PARTS, :], axis=0, keepdims=True)
    update_ref[...] = jnp.sum(lines[:count, :], axis=0, keepdims=True)


def middle_kernel(kept_ref, got_ref, base_ref, packed_ref):
    base_ref[...] = kept_ref[0] + got_ref[0]
    tile = kept_ref[1] + got_ref[1]
    rows, width = tile.shape
    packed_ref[:rows, :] = tile[:, :LANES].astype(jnp.bfloat16)
    rest = jnp.concatenate([tile[:, LANES:], jnp.zeros((4 * GROUP - rows, width - LANES), jnp.float32)], axis=0)
    pieces = [rest[at * GROUP : (at + 1) * GROUP, :] for at in range(4)]
    packed_ref[rows:, :] = jnp.concatenate(pieces, axis=1).astype(jnp.bfloat16)


def last_kernel(base_ref, packed_ref, tile_ref):
    rows, width = base_ref.shape
    side = width - LANES
    tile_ref[:, :LANES] = base_ref[:, :LANES] + packed_ref[:rows, :].astype(jnp.float32)
    rest = packed_ref[rows:, :].astype(jnp.float32)
    pieces = [rest[:, at * side : (at + 1) * side] for at in range(4)]
    tile_ref[:, LANES:] = base_ref[:, LANES:] + jnp.concatenate(pieces, axis=0)[:rows, :]


def swap(value, axis, bit):
    return lax.ppermute(value, axis, [(i, i ^ bit) for i in range(lax.axis_size(axis))])


def direct(derivatives, epsilon):
    n, m = lax.axis_size("smp"), lax.axis_size("par")
    rows, columns = derivatives.shape
    far = swap(derivatives, "smp", 4)
    own = pack(derivatives, epsilon)
    beside = swap(own, "smp", 2)
    other = swap(own, "smp", 1)
    far_beside = swap(far, "smp", 2)
    beside_other = swap(other, "smp", 2)
    far_other = swap(far, "smp", 1)
    far_beside_other = swap(far_beside, "smp", 1)
    near = (own, other, beside, beside_other)
    shapes = (jax.ShapeDtypeStruct((len(near) * EXTRA, LANES), jnp.bfloat16), jax.ShapeDtypeStruct((2, columns), jnp.float32))
    tails, early_sums = call(tails_kernel, shapes)(*near, far, far_beside)
    far_tails = swap(tails, "smp", 4)
    tile = jax.ShapeDtypeStruct((2, rows, rows * n // m), jnp.float32)
    lines = [pltpu.VMEM((n + SPARE, columns), jnp.float32)]
    sent, held = call(
        functools.partial(send_kernel, rows * n, (4, 6)),
        (tile, jax.ShapeDtypeStruct((n * rows, columns), jnp.bfloat16)),
        lines,
    )(early_sums, *near, far, far_other, far_beside, far_beside_other)
    got = swap(sent, "par", 1)
    kept = call(functools.partial(keep_kernel, rows), tile)(held)
    line = jax.ShapeDtypeStruct((1, columns), jnp.float32)
    update = call(functools.partial(update_kernel, rows), line, lines)(held, tails, far_tails)
    packed_rows = rows + GROUP
    base, packed = call(
        middle_kernel,
        (jax.ShapeDtypeStruct(tile.shape[1:], jnp.float32), jax.ShapeDtypeStruct((packed_rows, LANES), jnp.bfloat16)),
    )(kept, got)
    gram_tile = call(last_kernel, jax.ShapeDtypeStruct(tile.shape[1:], jnp.float32))(base, swap(packed, "par", 2))
    return (gram_tile, update.reshape(-1))


def gathered(derivatives, epsilon):
    total_rows = derivatives.shape[0] * lax.axis_size("smp")
    factor = 1.0 / math.sqrt(total_rows)
    everything = lax.all_gather(derivatives, "smp", axis=0, tiled=True)
    mean = jnp.sum(everything.astype(jnp.float32), axis=0) / total_rows
    own = centered(derivatives, mean, factor)
    partial_terms = jnp.dot(own, centered(everything, mean, factor).T, preferred_element_type=jnp.float32)
    gram_tile = lax.psum_scatter(partial_terms, "par", scatter_dimension=1, tiled=True)
    local_sum = jnp.dot(epsilon, own.astype(jnp.float32), precision=lax.Precision.HIGHEST)
    return (gram_tile, lax.psum(local_sum, "smp"))


def solution(mesh):
    in_specs = (P("smp", "par"), P("smp"))
    out_specs = (P("smp", "par"), P("par"))

    def shards(derivatives, epsilon):
        return (direct if small else gathered)(derivatives, epsilon)

    small = (mesh.shape["smp"], mesh.shape["par"]) == (8, 4)
    return jax.shard_map(shards, mesh=mesh, in_specs=in_specs, out_specs=out_specs, check_vma=False)
```
